32 devices in a mesh: sc: 16 (over z, y, x), cell: 2 (over core).
Axes of the slice: x: 2, y: 2, z: 4, core: 2. Of those that a mesh axis runs over, the one named last changes fastest.
Arguments:
- channel: bfloat16 [2, 32, 256, 256], P(None, 'sc', None, 'cell'), may hold values from -2 to 2
- data_letters: bfloat16 [2, 7, 1024, 256], P(None, None, 'sc'), may hold values from -4 to 4
- serving: int32 [256], replicated, may hold values from 0 to 3
- assigned_mask: int32 [32, 256], P('sc'), may hold values 0 or 1
Outputs:
- transmit: bfloat16 [2, 7, 1024, 256], P(None, None, 'sc', 'cell')
The draws below stay inside these ranges and needn't reach their ends.
All inputs are finite; a program needn't handle non-finite values. No bound on the sum of `assigned_mask` on one device may be relied on, other than what follows from the above.
Results may differ from the reference program's by a relative error of at most 0.0059.
Values may be sent and summed in bfloat16 or wider, within the bound.
A program may use at most 64 MiB of HBM per device.

```python
import math
import jax
import jax.numpy as jnp
from jax import lax

TERMINAL_SUM = 256
CELL_ANTENNAS = 64
TONES_PER_BUNDLE = 32
OFDM_SLOTS = 7
CELLS = 4
RADIATOR_SUM = 256
TONE_BUNDLES = 32
TONE_NUMBER = 1024


def draw_channel(key, part):
    gain_key = jax.random.fold_in(key, 11)
    fading_key = jax.random.fold_in(key, 12)
    tensor_layout = (2, TONE_BUNDLES, TERMINAL_SUM, RADIATOR_SUM)
    path_gains = jnp.exp(jax.random.uniform(gain_key, (TERMINAL_SUM, CELLS), jnp.float32, math.log(0.3), math.log(3.0)))
    fading_draw = jnp.clip(jax.random.normal(fading_key, tensor_layout, jnp.float32), -5.0, 5.0)
    delay_spread = jnp.repeat(path_gains, CELL_ANTENNAS, axis=1)
    return (fading_draw * delay_spread[None, None] / math.sqrt(2.0 * CELL_ANTENNAS)).astype(jnp.bfloat16)


def touch_ends(entries, own_key, low, top_value):
    dims = entries.shape
    place = [jax.random.randint(jax.random.fold_in(own_key, axis), (), 0, dims[axis]) for axis in range(len(dims))]
    entries = entries.at[tuple(place)].set(low)
    longest = dims.index(max(dims))
    place[longest] = (place[longest] + 1) % dims[longest]
    return entries.at[tuple(place)].set(top_value)


def level_of(key, extent, shards, least, high):
    level = 1.0
    for axis_at, parts in shards:
        draws = jax.random.uniform(jax.random.fold_in(jax.random.fold_in(key, 6), axis_at), (parts,), jnp.float32, least / len(shards), high / len(shards))
        level = level * jnp.repeat(jnp.exp(draws), extent[axis_at] // parts).reshape((-1,) + (1,) * (len(extent) - 1 - axis_at))
    return level


def centred(own_key, shape, width, bound, pieces=(), kind=jnp.bfloat16):
    array = width * jax.random.normal(own_key, shape, jnp.float32)
    if pieces:
        array = array * level_of(own_key, shape, pieces, -0.22, 0.18)
    return jnp.clip(array, -bound, bound).astype(kind)


def setup_inputs(seed: int = 0) -> dict:
    seeds = jax.random.split(jax.random.key(seed), 5)
    channel = draw_channel(jax.random.fold_in(seeds[4], 71), 0)
    data_letters = centred(seeds[1], (2, OFDM_SLOTS, TONE_NUMBER, TERMINAL_SUM), 0.7071, 4.0, ((2, 16),))
    serving = touch_ends(jax.random.randint(seeds[2], (TERMINAL_SUM,), 0, CELLS), jax.random.fold_in(seeds[2], 1), 0, CELLS - 1).astype(jnp.int32)
    assigned_mask = touch_ends((jax.random.randint(seeds[3], (TONE_BUNDLES, TERMINAL_SUM), 0, 4) < 3).astype(jnp.int32), jax.random.fold_in(seeds[3], 1), 0, 1)
    return dict(channel=channel, data_letters=data_letters, serving=serving, assigned_mask=assigned_mask)


NOISE = 0.1
REGUL = 0.5
CLIP_RATIO = 1.5
SMALL_FLOOR = 1e-06
HIGHEST = lax.Precision.HIGHEST

def product_partials(local_piece, serving, cell_width):
    antenna = jnp.arange(local_piece.shape[3], dtype=jnp.int32)
    served = ((antenna // cell_width)[None, :] == serving[:, None]).astype(jnp.float32)
    real_part = local_piece[0].astype(jnp.float32)
    imag_part = local_piece[1].astype(jnp.float32)
    own_real = real_part * served[None]
    own_imag = imag_part * served[None]
    stacked = jnp.concatenate([real_part, imag_part], axis=2)
    rotated = jnp.concatenate([imag_part, -real_part], axis=2)
    own_stack = jnp.concatenate([own_real, own_imag], axis=2)
    form = 'gkm,gjm->gkj'
    gramian_real = jnp.einsum(form, stacked, stacked, precision=HIGHEST)
    gramian_imag = jnp.einsum(form, rotated, stacked, precision=HIGHEST)
    product_real = jnp.einsum(form, stacked, own_stack, precision=HIGHEST)
    product_imag = jnp.einsum(form, rotated, own_stack, precision=HIGHEST)
    squared_magnitudes = lax.optimization_barrier(jnp.sum(own_stack * own_stack, axis=2))
    return (gramian_real, gramian_imag, product_real, product_imag, squared_magnitudes)

def solve_system(gramian_real, gramian_imag, eff_real, eff_imag, active):
    terminals = eff_real.shape[1]
    identity = jnp.eye(terminals, dtype=jnp.float32)
    power_terms = eff_real * eff_real + eff_imag * eff_imag
    overall = lax.optimization_barrier(jnp.sum(power_terms, axis=2)) + NOISE
    interference = lax.optimization_barrier(jnp.sum(power_terms * (1.0 - identity), axis=2)) + NOISE
    signal_real = lax.optimization_barrier(jnp.sum(eff_real * identity, axis=2))
    signal_imag = lax.optimization_barrier(jnp.sum(eff_imag * identity, axis=2))
    weight_root = jnp.sqrt(overall / interference)
    mix_real = weight_root * (signal_real / overall) * active
    mix_imag = -weight_root * (signal_imag / overall) * active
    left_real = mix_real[:, :, None] * gramian_real - mix_imag[:, :, None] * gramian_imag
    left_imag = mix_real[:, :, None] * gramian_imag + mix_imag[:, :, None] * gramian_real
    inner_real = left_real * mix_real[:, None, :] + left_imag * mix_imag[:, None, :] + REGUL * identity
    inner_imag = left_imag * mix_real[:, None, :] - left_real * mix_imag[:, None, :]
    system = jnp.concatenate([jnp.concatenate([inner_real, -inner_imag], axis=2), jnp.concatenate([inner_imag, inner_real], axis=2)], axis=1)
    right_side = jnp.concatenate([weight_root[:, :, None] * identity, jnp.zeros_like(inner_real)], axis=1)
    factor = jnp.linalg.cholesky(system)
    middle = jax.scipy.linalg.solve_triangular(factor, right_side, lower=True)
    solved = jax.scipy.linalg.solve_triangular(factor, middle, trans=1, lower=True)
    sol_real = solved[:, :terminals]
    sol_imag = solved[:, terminals:]
    coef_real = mix_real[:, :, None] * sol_real + mix_imag[:, :, None] * sol_imag
    coef_imag = mix_real[:, :, None] * sol_imag - mix_imag[:, :, None] * sol_real
    return (coef_real, coef_imag)

def precoder_rows(local_piece, coef_real, coef_imag):
    wide = local_piece.astype(jnp.float32)
    stacked = jnp.concatenate([wide[0], wide[1]], axis=1)
    first = jnp.concatenate([coef_real, coef_imag], axis=1)
    second = jnp.concatenate([coef_imag, -coef_real], axis=1)
    rows_real = jnp.einsum('gkm,gkj->gmj', stacked, first, precision=HIGHEST)
    rows_imag = jnp.einsum('gkm,gkj->gmj', stacked, second, precision=HIGHEST)
    return (rows_real, rows_imag)

def reference(channel, data_letters, serving, assigned_mask):

    def per_group(element_entry):
        group_channel, group_active = element_entry
        local_piece = group_channel[:, None]
        active = group_active[None].astype(jnp.float32)
        gramian_real, gramian_imag, product_real, product_imag, squared_magnitudes = product_partials(local_piece, serving, CELL_ANTENNAS)
        column_scale = active / jnp.sqrt(squared_magnitudes + SMALL_FLOOR)
        eff_real = product_real * column_scale[:, None, :]
        eff_imag = product_imag * column_scale[:, None, :]
        coef_real, coef_imag = solve_system(gramian_real, gramian_imag, eff_real, eff_imag, active)
        rows_real, rows_imag = precoder_rows(local_piece, coef_real, coef_imag)
        signal_strength = lax.optimization_barrier(jnp.sum(rows_real * rows_real + rows_imag * rows_imag, axis=(1, 2)))
        power_scale = jnp.sqrt(RADIATOR_SUM / (signal_strength + SMALL_FLOOR))[:, None, None]
        return jnp.stack([(rows_real * power_scale)[0], (rows_imag * power_scale)[0]]).astype(jnp.bfloat16)
    precoders = lax.map(per_group, (jnp.moveaxis(channel, 1, 0), assigned_mask))
    prec_real = precoders[:, 0].astype(jnp.float32)
    prec_imag = precoders[:, 1].astype(jnp.float32)
    square_radix = math.sqrt(TONE_NUMBER)

    def per_symbol(element_entry):
        bundled_tones = element_entry.astype(jnp.float32).reshape(2, TONE_BUNDLES, TONES_PER_BUNDLE, TERMINAL_SUM)
        form = 'gfk,gmk->gfm'
        emitted_inphase = jnp.einsum(form, bundled_tones[0], prec_real, precision=HIGHEST) - jnp.einsum(form, bundled_tones[1], prec_imag, precision=HIGHEST)
        emitted_quadrature = jnp.einsum(form, bundled_tones[0], prec_imag, precision=HIGHEST) + jnp.einsum(form, bundled_tones[1], prec_real, precision=HIGHEST)
        rounded_inphase = lax.optimization_barrier(emitted_inphase.reshape(TONE_NUMBER, RADIATOR_SUM).astype(jnp.bfloat16))
        rounded_quadrature = lax.optimization_barrier(emitted_quadrature.reshape(TONE_NUMBER, RADIATOR_SUM).astype(jnp.bfloat16))
        spectrum = rounded_inphase.astype(jnp.float32) + 1j * rounded_quadrature.astype(jnp.float32)
        timeline = jnp.fft.ifft(spectrum, axis=0) * square_radix
        power = jnp.real(timeline) ** 2 + jnp.imag(timeline) ** 2
        limit = CLIP_RATIO * jnp.sqrt(lax.optimization_barrier(jnp.mean(power, axis=0)) + SMALL_FLOOR)
        clipped = timeline * (limit / jnp.sqrt(jnp.maximum(power, limit * limit)))
        back = jnp.fft.fft(clipped, axis=0) / square_radix
        return jnp.stack([jnp.real(back), jnp.imag(back)]).astype(jnp.bfloat16)
    result = lax.map(per_symbol, jnp.moveaxis(data_letters, 1, 0))
    return jnp.moveaxis(result, 0, 1)
```

```python
import functools
import math

import jax
import jax.numpy as jnp
import numpy as np
from jax import lax
from jax.experimental import pallas as pl
from jax.experimental.pallas import tpu as pltpu
from jax.sharding import PartitionSpec as P

CELL_ANTENNAS = 64
NOISE = 0.1
REGUL = 0.5
CLIP_RATIO = 1.5
SMALL_FLOOR = 1e-06
HIGHEST = lax.Precision.HIGHEST
F32 = jnp.float32
BF16 = jnp.bfloat16
HALF = 64
RADIX = 256


def nt(left, right):
    return lax.dot_general(
        left, right, (((1,), (1,)), ((), ())), preferred_element_type=F32
    )


def mm(left, right):
    return jnp.dot(left, right, preferred_element_type=F32)


def mm_full(left, right):
    return jnp.dot(left, right, preferred_element_type=F32, precision=HIGHEST)


def split(value):
    high = value.astype(BF16)
    return high, (value - high.astype(F32)).astype(BF16)


def complex_low(ar, ai, br, bi):
    a = jnp.concatenate([ar.astype(BF16), ai.astype(BF16)], axis=0)
    u = mm(a, br.astype(BF16))
    v = mm(a, bi.astype(BF16))
    n = ar.shape[0]
    return u[:n] - v[n:], u[n:] + v[:n]


def complex_full(ar, ai, br, bi):
    return (
        mm_full(ar, br) - mm_full(ai, bi),
        mm_full(ar, bi) + mm_full(ai, br),
    )


def newton_step(product, br, bi, xr, xi, eye, scale):
    yr = xr * scale
    yi = xi * scale
    tr, ti = product(br, bi, yr, yi)
    rr = eye - tr
    ri = -ti
    dr, di = product(yr, yi, rr, ri)
    return yr + dr, yi + di, rr, ri


def precode_kernel(pieces, cell_width, own_ref, other_ref, data_ref, serving_ref, mask_ref, send_ref):
    me = lax.axis_index("cell")
    users = own_ref.shape[2]
    width = own_ref.shape[3]
    serving = serving_ref[...]
    real_list, imag_list, own_real, own_imag = [], [], [], []
    for i in range(pieces):
        piece = own_ref[:, 0] if i == 0 else other_ref[i - 1, :, 0]
        start = lax.rem(me + i, pieces) * width
        antenna = start + lax.broadcasted_iota(jnp.int32, (users, width), 1)
        served = (antenna // cell_width) == serving
        zero = jnp.zeros((users, width), BF16)
        real_list.append(piece[0])
        imag_list.append(piece[1])
        own_real.append(jnp.where(served, piece[0].astype(F32), 0.0).astype(BF16))
        own_imag.append(jnp.where(served, piece[1].astype(F32), 0.0).astype(BF16))
    hr = jnp.concatenate(real_list, axis=1)
    hi = jnp.concatenate(imag_list, axis=1)
    por = jnp.concatenate(own_real, axis=1)
    poi = jnp.concatenate(own_imag, axis=1)
    gram_r = nt(hr, hr) + nt(hi, hi)
    cross = nt(hi, hr)
    gram_i = cross - nt(hr, hi)
    prod_r = nt(hr, por) + nt(hi, poi)
    prod_i = nt(hi, por) - nt(hr, poi)
    row = lax.broadcasted_iota(jnp.int32, (users, users), 0)
    col = lax.broadcasted_iota(jnp.int32, (users, users), 1)
    diagonal = row == col
    eye = diagonal.astype(F32)

    def to_row(column):
        return jnp.sum(eye * column, axis=0, keepdims=True)

    def to_column(line):
        return jnp.sum(eye * line, axis=1, keepdims=True)

    active_row = mask_ref[0].astype(F32)
    active_col = to_column(active_row)
    size_row = jnp.sum(prod_r * eye, axis=0, keepdims=True)
    col_scale = active_row / jnp.sqrt(size_row + SMALL_FLOOR)
    eff_r = prod_r * col_scale
    eff_i = prod_i * col_scale
    power = eff_r * eff_r + eff_i * eff_i
    overall = jnp.sum(power, axis=1, keepdims=True) + NOISE
    interference = jnp.sum(jnp.where(diagonal, 0.0, power), axis=1, keepdims=True) + NOISE
    direct = jnp.sum(eff_r * eye, axis=1, keepdims=True)
    weight_root = jnp.sqrt(overall / interference)
    mix = weight_root * (direct / overall) * active_col
    mix_row = to_row(mix)
    gram_diag = jnp.sum(gram_r * eye, axis=1, keepdims=True)
    inner_diag = mix * mix * gram_diag + REGUL
    unit = lax.rsqrt(inner_diag)
    left = mix * unit
    right = to_row(left)
    br = jnp.where(diagonal, 1.0, gram_r * left * right)
    bi = gram_i * left * right
    upper = jnp.max(jnp.sum(jnp.abs(br) + jnp.abs(bi), axis=1, keepdims=True))
    lower = REGUL / jnp.max(inner_diag)
    mild = lower > 0.01 * upper

    xr = eye
    xi = jnp.zeros_like(eye)

    def bound_after(low, high):
        spread = (high - low) / (high + low)
        return 1.0 - spread * spread

    def quick_cond(state):
        return jnp.logical_and(mild, 1.0 - state[0] / state[1] > 0.004)

    def quick_body(state):
        low, high, xr, xi = state
        xr, xi, _, _ = newton_step(complex_low, br, bi, xr, xi, eye, 2.0 / (low + high))
        return bound_after(low, high), jnp.float32(1.0), xr, xi

    low, high, xr, xi = lax.while_loop(quick_cond, quick_body, (lower, upper, xr, xi))
    low = jnp.where(mild, 1.0, low)
    high = jnp.where(mild, 1.0, high)

    def full_cond(state):
        return jnp.logical_and(state[2] > 0.003, state[3] < 40)

    def full_body(state):
        low, high, _, count, xr, xi = state
        xr, xi, rr, ri = newton_step(
            complex_full, br, bi, xr, xi, eye, 2.0 / (low + high)
        )
        left_over = jnp.sum(rr * rr + ri * ri)
        near = bound_after(low, high)
        return near, jnp.float32(1.0), left_over, count + 1, xr, xi

    _, _, _, _, xr, xi = lax.while_loop(
        full_cond, full_body, (low, high, jnp.float32(1.0), jnp.int32(0), xr, xi)
    )
    front = weight_root * unit
    yr_high, yr_low = split(xr * front * right)
    yi_high, yi_low = split(xi * front * right)
    qr = (mm(yr_high, hr) - mm(yi_high, hi)) + (mm(yr_low, hr) - mm(yi_low, hi))
    qi = (mm(yr_high, hi) + mm(yi_high, hr)) + (mm(yr_low, hi) + mm(yi_low, hr))
    strength = jnp.sum(qr * qr + qi * qi, keepdims=True)
    scale = jnp.sqrt((pieces * width) / (strength + SMALL_FLOOR))
    pr = (qr[:, :width] * scale).astype(BF16)
    pi = (qi[:, :width] * -scale).astype(BF16)
    top, bottom = [], []
    for h in range(width // HALF):
        cut = slice(h * HALF, (h + 1) * HALF)
        top += [pr[:, cut], pi[:, cut]]
        bottom += [-pi[:, cut], pr[:, cut]]
    top = jnp.concatenate(top, axis=1)
    bottom = jnp.concatenate(bottom, axis=1)
    slots = data_ref.shape[1]
    tones = data_ref.shape[2]
    letters_r = data_ref[0].reshape(slots * tones, users)
    letters_i = data_ref[1].reshape(slots * tones, users)
    signal = (mm(letters_r, top) + mm(letters_i, bottom)).astype(BF16)
    halves = width // HALF
    for s in range(slots):
        for h in range(halves):
            send_ref[s * halves + h] = signal[
                s * tones : (s + 1) * tones, h * 2 * HALF : (h + 1) * 2 * HALF
            ]
    for d in range(slots * halves, send_ref.shape[0]):
        send_ref[d] = jnp.zeros(send_ref.shape[1:], BF16)


def precode(channel, others, data_letters, serving, mask, parts, pieces):
    groups = channel.shape[1]
    users = channel.shape[2]
    width = channel.shape[3]
    slots = data_letters.shape[1]
    tones = data_letters.shape[2]
    per = tones // groups
    return pl.pallas_call(
        functools.partial(precode_kernel, pieces, CELL_ANTENNAS),
        grid=(groups,),
        out_shape=jax.ShapeDtypeStruct((parts, tones, 2 * HALF), BF16),
        in_specs=[
            pl.BlockSpec((2, 1, users, width), lambda g: (0, g, 0, 0)),
            pl.BlockSpec((pieces - 1, 2, 1, users, width), lambda g: (0, 0, g, 0, 0)),
            pl.BlockSpec((2, slots, per, users), lambda g: (0, 0, g, 0)),
            pl.BlockSpec((users, 1), lambda g: (0, 0)),
            pl.BlockSpec((1, 1, users), lambda g: (g, 0, 0)),
        ],
        out_specs=pl.BlockSpec((parts, per, 2 * HALF), lambda g: (0, g, 0)),
        compiler_params=pltpu.CompilerParams(vmem_limit_bytes=48 * 1024 * 1024),
        name="precode",
    )(channel, others, data_letters, serving, mask)


def fft_tables(length):
    radix = length // RADIX
    q = np.arange(RADIX)
    back, forth = [], []
    for n1 in range(radix):
        angle = 2.0 * np.pi * ((q[:, None] * (radix * q[None, :] + n1)) % length) / length
        cos, sin = np.cos(angle), np.sin(angle)
        back.append(np.concatenate([cos.T, sin.T], axis=0))
        forth.append(np.concatenate([cos, sin], axis=0))
    return (
        jnp.asarray(np.stack(back), BF16),
        jnp.asarray(np.stack(forth), BF16),
    )


def weighted(values, turned, radix, n, sign):
    total = None
    for r in range(radix):
        step = (r * n) % radix
        cos = math.cos(2.0 * math.pi * step / radix)
        sin = sign * math.sin(2.0 * math.pi * step / radix)
        for factor, piece in ((cos, values[r]), (sin, turned[r])):
            if abs(factor) < 1e-9:
                continue
            if abs(factor - 1.0) < 1e-9:
                term = piece
            elif abs(factor + 1.0) < 1e-9:
                term = -piece
            else:
                term = factor * piece
            total = term if total is None else total + term
    return total


def fft_kernel(length, in_ref, back_ref, forth_ref, out_ref):
    radix = length // RADIX
    lanes = 2 * HALF
    sign = jnp.where(
        lax.broadcasted_iota(jnp.int32, (RADIX, lanes), 1) < HALF, -1.0, 1.0
    )

    def turn(value):
        return pltpu.roll(value, HALF, 1) * sign

    norm = 1.0 / math.sqrt(length)
    blocks = [in_ref[pl.ds(r * RADIX, RADIX), :].astype(F32) for r in range(radix)]
    turned = [turn(b) for b in blocks]
    waves, powers = [], []
    energy = jnp.zeros((1, lanes), F32)
    for n in range(radix):
        mixed = weighted(blocks, turned, radix, n, 1.0).astype(BF16)
        both = mm(back_ref[n], mixed)
        wave = (both[:RADIX] + turn(both[RADIX:])) * norm
        square = wave * wave
        power = square + pltpu.roll(square, HALF, 1)
        energy = energy + jnp.sum(power, axis=0, keepdims=True)
        waves.append(wave)
        powers.append(power)
    limit_square = CLIP_RATIO * CLIP_RATIO * (energy * (1.0 / length) + SMALL_FLOOR)
    limit = jnp.sqrt(limit_square) * norm
    spectra = []
    for n in range(radix):
        clipped = waves[n] * (limit * lax.rsqrt(jnp.maximum(powers[n], limit_square)))
        both = mm(forth_ref[n], clipped.astype(BF16))
        spectra.append(both[:RADIX] - turn(both[RADIX:]))
    turned = [turn(b) for b in spectra]
    for r in range(radix):
        out_ref[pl.ds(r * RADIX, RADIX), :] = weighted(
            spectra, turned, radix, r, -1.0
        ).astype(BF16)


def transform(block):
    length = block.shape[0]
    back, forth = fft_tables(length)
    return pl.pallas_call(
        functools.partial(fft_kernel, length),
        out_shape=jax.ShapeDtypeStruct(block.shape, BF16),
        compiler_params=pltpu.CompilerParams(vmem_limit_bytes=48 * 1024 * 1024),
        name="transform",
    )(block, back, forth)


def spread_kernel(halves, in_ref, out_ref):
    for s in range(out_ref.shape[1]):
        pieces = [in_ref[s * halves + h] for h in range(halves)]
        for c in range(2):
            out_ref[c, s] = jnp.concatenate(
                [p[:, c * HALF : (c + 1) * HALF] for p in pieces], axis=1
            )


def spread(received, slots, width):
    tones = received.shape[1]
    return pl.pallas_call(
        functools.partial(spread_kernel, width // HALF),
        out_shape=jax.ShapeDtypeStruct((2, slots, tones, width), BF16),
        name="spread",
    )(received)


def body(channel, data_letters, serving, assigned_mask):
    parts = lax.axis_size("sc")
    pieces = lax.axis_size("cell")
    others = jnp.stack(
        [
            lax.ppermute(channel, "cell", [((i + k) % pieces, i) for i in range(pieces)])
            for k in range(1, pieces)
        ]
    )
    send = precode(
        channel,
        others,
        data_letters,
        serving[:, None],
        assigned_mask[:, None, :],
        parts,
        pieces,
    )
    tones = send.shape[1]
    gathered = lax.all_to_all(send, "sc", split_axis=0, concat_axis=0, tiled=True)
    spectrum = transform(gathered.reshape(parts * tones, 2 * HALF))
    back = lax.all_to_all(
        spectrum.reshape(parts, tones, 2 * HALF), "sc", split_axis=0, concat_axis=0, tiled=True
    )
    return spread(back, data_letters.shape[1], channel.shape[3])


def solution(mesh):
    return jax.shard_map(
        body,
        mesh=mesh,
        in_specs=(P(None, "sc", None, "cell"), P(None, None, "sc", None), P(), P("sc", None)),
        out_specs=P(None, None, "sc", "cell"),
        check_vma=False,
    )
```

```python
import functools
import math

import jax
import jax.numpy as jnp
import numpy as np
from jax import lax
from jax.experimental import pallas as pl
from jax.experimental.pallas import tpu as pltpu
from jax.sharding import PartitionSpec as P

CELL_ANTENNAS = 64
NOISE = 0.1
REGUL = 0.5
CLIP_RATIO = 1.5
SMALL_FLOOR = 1e-06
HIGHEST = lax.Precision.HIGHEST
F32 = jnp.float32
BF16 = jnp.bfloat16
HALF = 64
RADIX = 256


def nt(left, right):
    return lax.dot_general(
        left, right, (((1,), (1,)), ((), ())), preferred_element_type=F32
    )


def mm(left, right):
    return jnp.dot(left, right, preferred_element_type=F32)


def mm_full(left, right):
    return jnp.dot(left, right, preferred_element_type=F32, precision=HIGHEST)


def split(value):
    high = value.astype(BF16)
    return high, (value - high.astype(F32)).astype(BF16)


def complex_low(ar, ai, br, bi):
    a = jnp.concatenate([ar.astype(BF16), ai.astype(BF16)], axis=0)
    u = mm(a, br.astype(BF16))
    v = mm(a, bi.astype(BF16))
    n = ar.shape[0]
    return u[:n] - v[n:], u[n:] + v[:n]


def complex_split(ar, ai, br, bi):
    ar_high, ar_low = split(ar)
    ai_high, ai_low = split(ai)
    br_high, br_low = split(br)
    bi_high, bi_low = split(bi)
    n = ar.shape[0]
    a = jnp.concatenate([ar_high, ai_high, ar_low, ai_low], axis=0)
    a_high = jnp.concatenate([ar_high, ai_high], axis=0)
    u = mm(a, br_high)
    v = mm(a, bi_high)
    u_low = mm(a_high, br_low)
    v_low = mm(a_high, bi_low)
    rr = u[2 * n : 3 * n] + u_low[:n]
    ir = u[3 * n :] + u_low[n:]
    ri = v[2 * n : 3 * n] + v_low[:n]
    ii = v[3 * n :] + v_low[n:]
    return (u[:n] - v[n : 2 * n]) + (rr - ii), (u[n : 2 * n] + v[:n]) + (ir + ri)


def complex_full(ar, ai, br, bi):
    return (
        mm_full(ar, br) - mm_full(ai, bi),
        mm_full(ar, bi) + mm_full(ai, br),
    )


def newton_step(first, second, br, bi, xr, xi, eye, scale):
    yr = xr * scale
    yi = xi * scale
    tr, ti = first(br, bi, yr, yi)
    rr = eye - tr
    ri = -ti
    dr, di = second(yr, yi, rr, ri)
    return yr + dr, yi + di, rr, ri


def bound_after(low, high):
    spread = (high - low) / (high + low)
    return 1.0 - spread * spread


def precode_kernel(pieces, cell_width, shared, own_ref, other_ref, serving_ref, mask_ref, mine_ref, *theirs_ref):
    me = lax.axis_index("cell")
    at = me if shared else 0
    group = me if shared else pl.program_id(0)
    users = own_ref.shape[2]
    width = own_ref.shape[3]
    row = lax.broadcasted_iota(jnp.int32, (users, users), 0)
    col = lax.broadcasted_iota(jnp.int32, (users, users), 1)
    diagonal = row == col
    eye = diagonal.astype(F32)

    def to_row(column):
        return jnp.sum(eye * column, axis=0, keepdims=True)

    def to_column(line):
        return jnp.sum(eye * line, axis=1, keepdims=True)

    serving = to_column(serving_ref[...].astype(F32))
    real_list, imag_list, own_real, own_imag = [], [], [], []
    for i in range(pieces):
        real = own_ref[0, at] if i == 0 else other_ref[i - 1, 0, at]
        imag = own_ref[1, at] if i == 0 else other_ref[i - 1, 1, at]
        start = lax.rem(me + i, pieces) * width
        antenna = start + lax.broadcasted_iota(jnp.int32, (users, width), 1)
        served = (antenna // cell_width).astype(F32) == serving
        real_list.append(real)
        imag_list.append(imag)
        own_real.append(jnp.where(served, real.astype(F32), 0.0).astype(BF16))
        own_imag.append(jnp.where(served, imag.astype(F32), 0.0).astype(BF16))
    hr = jnp.concatenate(real_list, axis=1)
    hi = jnp.concatenate(imag_list, axis=1)
    por = jnp.concatenate(own_real, axis=1)
    poi = jnp.concatenate(own_imag, axis=1)
    prod_r = nt(hr, por) + nt(hi, poi)
    prod_i = nt(hi, por) - nt(hr, poi)
    gram_r = nt(hr, hr) + nt(hi, hi)
    gram_i = nt(hi, hr) - nt(hr, hi)
    active_row = mask_ref[pl.ds(group, 1), :].astype(F32)
    active_col = to_column(active_row)
    size_row = jnp.sum(prod_r * eye, axis=0, keepdims=True)
    col_scale = active_row / jnp.sqrt(size_row + SMALL_FLOOR)
    eff_r = prod_r * col_scale
    eff_i = prod_i * col_scale
    power = eff_r * eff_r + eff_i * eff_i
    overall = jnp.sum(power, axis=1, keepdims=True) + NOISE
    interference = jnp.sum(jnp.where(diagonal, 0.0, power), axis=1, keepdims=True) + NOISE
    direct = jnp.sum(eff_r * eye, axis=1, keepdims=True)
    weight_root = jnp.sqrt(overall / interference)
    mix = weight_root * (direct / overall) * active_col
    gram_diag = jnp.sum(gram_r * eye, axis=1, keepdims=True)
    inner_diag = mix * mix * gram_diag + REGUL
    unit = lax.rsqrt(inner_diag)
    left = mix * unit
    right = to_row(left)
    br = jnp.where(diagonal, 1.0, gram_r * left * right)
    bi = gram_i * left * right
    upper = jnp.max(jnp.sum(jnp.sqrt(br * br + bi * bi), axis=1, keepdims=True))
    lower = REGUL / jnp.max(inner_diag)
    mild = lower > 0.01 * upper

    scale = 2.0 / (lower + upper)
    xr = scale * (2.0 * eye - scale * br)
    xi = -scale * scale * bi

    def quick_cond(state):
        return jnp.logical_and(mild, 1.0 - state[0] > 0.02)

    def quick_body(state):
        low, xr, xi = state
        xr, xi, _, _ = newton_step(
            complex_low, complex_low, br, bi, xr, xi, eye, 2.0 / (low + 1.0)
        )
        return bound_after(low, 1.0), xr, xi

    low, xr, xi = lax.while_loop(quick_cond, quick_body, (bound_after(lower, upper), xr, xi))
    low = jnp.where(mild, 1.0, low)

    def close_cond(state):
        return jnp.logical_and(mild, jnp.logical_and(state[0] > 0.003, state[1] < 3))

    def close_body(state):
        _, count, xr, xi = state
        xr, xi, rr, ri = newton_step(
            complex_split, complex_low, br, bi, xr, xi, eye, 1.0
        )
        return jnp.sum(rr * rr + ri * ri), count + 1, xr, xi

    remains, _, xr, xi = lax.while_loop(
        close_cond, close_body, (jnp.float32(1.0), jnp.int32(0), xr, xi)
    )

    def full_cond(state):
        return jnp.logical_and(state[1] > 0.003, state[2] < 40)

    def full_body(state):
        low, _, count, xr, xi = state
        xr, xi, rr, ri = newton_step(
            complex_full, complex_full, br, bi, xr, xi, eye, 2.0 / (low + 1.0)
        )
        return bound_after(low, 1.0), jnp.sum(rr * rr + ri * ri), count + 1, xr, xi

    _, _, _, xr, xi = lax.while_loop(
        full_cond, full_body, (low, remains, jnp.int32(0), xr, xi)
    )
    front = weight_root * unit
    yr_high, yr_low = split(xr * front * right)
    yi_high, yi_low = split(xi * front * right)
    qr = (mm(yr_high, hr) - mm(yi_high, hi)) + (mm(yr_low, hr) - mm(yi_low, hi))
    qi = (mm(yr_high, hi) + mm(yi_high, hr)) + (mm(yr_low, hi) + mm(yi_low, hr))
    strength = jnp.sum(qr * qr + qi * qi, keepdims=True)
    scale = jnp.sqrt((pieces * width) / (strength + SMALL_FLOOR))
    pr = (qr * scale).astype(BF16)
    pi = (qi * -scale).astype(BF16)
    mine_ref[0, 0] = pr[:, :width]
    mine_ref[0, 1] = pi[:, :width]
    if shared:
        theirs_ref[0][0] = pr[:, width:]
        theirs_ref[0][1] = pi[:, width:]


def precode(channel, others, serving, mask, pieces, shared):
    groups = channel.shape[1]
    users = channel.shape[2]
    width = channel.shape[3]
    params = pltpu.CompilerParams(vmem_limit_bytes=40 * 1024 * 1024)
    kernel = functools.partial(precode_kernel, pieces, CELL_ANTENNAS, shared)
    if shared:
        whole = pl.BlockSpec(memory_space=pltpu.VMEM)
        return pl.pallas_call(
            kernel,
            out_shape=(
                jax.ShapeDtypeStruct((1, 2, users, width), BF16),
                jax.ShapeDtypeStruct((2, users, width), BF16),
            ),
            in_specs=[whole] * 4,
            out_specs=(whole, whole),
            compiler_params=params,
            name="precode",
        )(channel, others, serving, mask)
    mine = pl.pallas_call(
        kernel,
        grid=(groups,),
        out_shape=jax.ShapeDtypeStruct((groups, 2, users, width), BF16),
        in_specs=[
            pl.BlockSpec((2, 1, users, width), lambda g: (0, g, 0, 0)),
            pl.BlockSpec((pieces - 1, 2, 1, users, width), lambda g: (0, 0, g, 0, 0)),
            pl.BlockSpec((1, users), lambda g: (0, 0)),
            pl.BlockSpec((groups, users), lambda g: (0, 0)),
        ],
        out_specs=pl.BlockSpec((1, 2, users, width), lambda g: (g, 0, 0, 0)),
        compiler_params=params,
        name="precode",
    )(channel, others, serving, mask)
    return mine, mine[0]


def fft_tables(length):
    radix = length // RADIX
    q = np.arange(RADIX)
    back, forth = [], []
    for n1 in range(radix):
        angle = 2.0 * np.pi * ((q[:, None] * (radix * q[None, :] + n1)) % length) / length
        cos, sin = np.cos(angle), np.sin(angle)
        back.append(np.concatenate([cos.T, sin.T], axis=0))
        forth.append(np.concatenate([cos, sin], axis=0))
    return (
        jnp.asarray(np.stack(back), BF16),
        jnp.asarray(np.stack(forth), BF16),
    )


def weighted(values, turned, radix, n, sign):
    total = None
    for r in range(radix):
        step = (r * n) % radix
        cos = math.cos(2.0 * math.pi * step / radix)
        sin = sign * math.sin(2.0 * math.pi * step / radix)
        for factor, piece in ((cos, values[r]), (sin, turned[r])):
            if abs(factor) < 1e-9:
                continue
            if abs(factor - 1.0) < 1e-9:
                term = piece
            elif abs(factor + 1.0) < 1e-9:
                term = -piece
            else:
                term = factor * piece
            total = term if total is None else total + term
    return total


def clip_transform(length, in_ref, back_ref, forth_ref, out_ref):
    radix = length // RADIX
    lanes = 2 * HALF
    sign = jnp.where(
        lax.broadcasted_iota(jnp.int32, (RADIX, lanes), 1) < HALF, -1.0, 1.0
    )

    def turn(value):
        return pltpu.roll(value, HALF, 1) * sign

    norm = 1.0 / math.sqrt(length)
    blocks = [in_ref[pl.ds(r * RADIX, RADIX), :].astype(F32) for r in range(radix)]
    turned = [turn(b) for b in blocks]
    waves, powers = [], []
    energy = jnp.zeros((1, lanes), F32)
    for n in range(radix):
        mixed = weighted(blocks, turned, radix, n, 1.0).astype(BF16)
        both = mm(back_ref[n], mixed)
        wave = (both[:RADIX] + turn(both[RADIX:])) * norm
        square = wave * wave
        power = square + pltpu.roll(square, HALF, 1)
        energy = energy + jnp.sum(power, axis=0, keepdims=True)
        waves.append(wave)
        powers.append(power)
    limit_square = CLIP_RATIO * CLIP_RATIO * (energy * (1.0 / length) + SMALL_FLOOR)
    limit = jnp.sqrt(limit_square) * norm
    spectra = []
    for n in range(radix):
        clipped = waves[n] * (limit * lax.rsqrt(jnp.maximum(powers[n], limit_square)))
        both = mm(forth_ref[n], clipped.astype(BF16))
        spectra.append(both[:RADIX] - turn(both[RADIX:]))
    turned = [turn(b) for b in spectra]
    for r in range(radix):
        out_ref[pl.ds(r * RADIX, RADIX), :] = weighted(
            spectra, turned, radix, r, -1.0
        ).astype(BF16)


def exchange_kernel(
    parts,
    shared,
    mine_ref,
    theirs_ref,
    data_ref,
    back_ref,
    forth_ref,
    out_ref,
    other_ref,
    send_ref,
    recv_ref,
    spec_ref,
    ret_ref,
    swap_sems,
    send_sems,
    recv_sems,
    back_send,
    back_recv,
):
    me = lax.axis_index("sc")
    core = lax.axis_index("cell")
    length = recv_ref.shape[0]
    active = send_ref.shape[0]
    slots = data_ref.shape[1]
    tones = data_ref.shape[2]
    users = data_ref.shape[3]
    width = mine_ref.shape[3]
    halves = width // HALF
    groups = 2 if shared else mine_ref.shape[0]
    per = tones // groups
    mesh_ids = pl.DeviceIdType.MESH
    barrier = pltpu.get_barrier_semaphore()

    @pl.loop(1, parts)
    def _(k):
        pl.semaphore_signal(
            barrier, inc=1, device_id=(lax.rem(me + k, parts), core), device_id_type=mesh_ids
        )

    if shared:
        pl.semaphore_signal(barrier, inc=1, device_id=(me, 1 - core), device_id_type=mesh_ids)

    def emit(group, pr, pi):
        top, bottom = [], []
        for h in range(halves):
            cut = slice(h * HALF, (h + 1) * HALF)
            top += [pr[:, cut], pi[:, cut]]
            bottom += [-pi[:, cut], pr[:, cut]]
        top = jnp.concatenate(top, axis=1)
        bottom = jnp.concatenate(bottom, axis=1)
        start = pl.multiple_of(group * per, per)
        letters_r = data_ref[0, :, pl.ds(start, per), :].reshape(slots * per, users)
        letters_i = data_ref[1, :, pl.ds(start, per), :].reshape(slots * per, users)
        signal = (mm(letters_r, top) + mm(letters_i, bottom)).astype(BF16)
        for s in range(slots):
            for h in range(halves):
                send_ref[s * halves + h, pl.ds(start, per), :] = signal[
                    s * per : (s + 1) * per, h * 2 * HALF : (h + 1) * 2 * HALF
                ]

    def outward(group, target, origin):
        start = pl.multiple_of(group * per, per)
        place = pl.multiple_of(origin * tones + group * per, per)
        return pltpu.make_async_remote_copy(
            src_ref=send_ref.at[target, pl.ds(start, per)],
            dst_ref=recv_ref.at[pl.ds(place, per)],
            send_sem=send_sems.at[group, target],
            recv_sem=recv_sems.at[group, origin],
            device_id=(target, core),
            device_id_type=mesh_ids,
        )

    def send_group(group):
        @pl.loop(1, parts)
        def _(k):
            target = lax.rem(me + k, parts)

            @pl.when(target < active)
            def _():
                outward(group, target, me).start()

        @pl.when(me < active)
        def _():
            start = pl.multiple_of(group * per, per)
            place = pl.multiple_of(me * tones + group * per, per)
            recv_ref[pl.ds(place, per), :] = send_ref[me, pl.ds(start, per), :]

    if shared:
        emit(core, mine_ref[0, 0], mine_ref[0, 1])
        pl.semaphore_wait(barrier, parts)
        swap = pltpu.make_async_remote_copy(
            src_ref=theirs_ref,
            dst_ref=other_ref,
            send_sem=swap_sems.at[0],
            recv_sem=swap_sems.at[1],
            device_id=(me, 1 - core),
            device_id_type=mesh_ids,
        )
        swap.start()
        send_group(core)
        swap.wait()
        emit(1 - core, other_ref[0], other_ref[1])
        send_group(1 - core)
    else:
        for g in range(groups):
            emit(g, mine_ref[g, 0], mine_ref[g, 1])
        pl.semaphore_wait(barrier, parts - 1)
        for g in range(groups):
            send_group(g)

    def homeward(target, origin):
        place = pl.multiple_of(target * tones, tones)
        return pltpu.make_async_remote_copy(
            src_ref=spec_ref.at[pl.ds(place, tones)],
            dst_ref=ret_ref.at[origin],
            send_sem=back_send.at[target],
            recv_sem=back_recv.at[origin],
            device_id=(target, core),
            device_id_type=mesh_ids,
        )

    @pl.when(me < active)
    def _():
        @pl.loop(1, parts)
        def _(k):
            origin = lax.rem(me + k, parts)
            for g in range(groups):
                outward(g, me, origin).wait_recv()

        clip_transform(length, recv_ref, back_ref, forth_ref, spec_ref)

        @pl.loop(1, parts)
        def _(k):
            homeward(lax.rem(me + k, parts), me).start()

        ret_ref[me] = spec_ref[pl.ds(pl.multiple_of(me * tones, tones), tones), :]

    for s in range(slots):
        for h in range(halves):

            @pl.when(me != s * halves + h)
            def _():
                homeward(me, s * halves + h).wait_recv()

        pieces = [ret_ref[s * halves + h] for h in range(halves)]
        for c in range(2):
            out_ref[c, s] = jnp.concatenate(
                [p[:, c * HALF : (c + 1) * HALF] for p in pieces], axis=1
            )

    @pl.loop(1, parts)
    def _(k):
        target = lax.rem(me + k, parts)

        @pl.when(target < active)
        def _():
            for g in range(groups):
                outward(g, target, me).wait_send()

        @pl.when(me < active)
        def _():
            homeward(target, me).wait_send()


def exchange(mine, theirs, data_letters, parts, shared):
    slots, tones = data_letters.shape[1], data_letters.shape[2]
    width = mine.shape[3]
    length = parts * tones
    active = slots * (width // HALF)
    groups = 2 if shared else mine.shape[0]
    back, forth = fft_tables(length)
    whole = pl.BlockSpec(memory_space=pltpu.VMEM)
    dma = pltpu.SemaphoreType.DMA
    return pl.pallas_call(
        functools.partial(exchange_kernel, parts, shared),
        out_shape=jax.ShapeDtypeStruct((2, slots, tones, width), BF16),
        in_specs=[whole] * 5,
        out_specs=whole,
        scratch_shapes=[
            pltpu.VMEM(theirs.shape, BF16),
            pltpu.VMEM((active, tones, 2 * HALF), BF16),
            pltpu.VMEM((length, 2 * HALF), BF16),
            pltpu.VMEM((length, 2 * HALF), BF16),
            pltpu.VMEM((active, tones, 2 * HALF), BF16),
            dma((2,)),
            dma((groups, active)),
            dma((groups, parts)),
            dma((parts,)),
            dma((active,)),
        ],
        compiler_params=pltpu.CompilerParams(
            collective_id=0, has_side_effects=True, vmem_limit_bytes=40 * 1024 * 1024
        ),
        name="exchange",
    )(mine, theirs, data_letters, back, forth)


def body(channel, data_letters, serving, assigned_mask):
    parts = lax.axis_size("sc")
    pieces = lax.axis_size("cell")
    shared = pieces == 2 and channel.shape[1] == 2
    others = [
        lax.ppermute(channel, "cell", [((i + k) % pieces, i) for i in range(pieces)])
        for k in range(1, pieces)
    ]
    mine, theirs = precode(
        channel, jnp.stack(others), serving[None, :], assigned_mask, pieces, shared
    )
    return exchange(mine, theirs, data_letters, parts, shared)


def solution(mesh):
    return jax.shard_map(
        body,
        mesh=mesh,
        in_specs=(P(None, "sc", None, "cell"), P(None, None, "sc", None), P(), P("sc", None)),
        out_specs=P(None, None, "sc", "cell"),
        check_vma=False,
    )
```

```python
import functools
import math

import jax
import jax.numpy as jnp
import numpy as np
from jax import lax
from jax.experimental import pallas as pl
from jax.experimental.pallas import tpu as pltpu
from jax.sharding import PartitionSpec as P

CELL_ANTENNAS = 64
NOISE = 0.1
REGUL = 0.5
CLIP_RATIO = 1.5
SMALL_FLOOR = 1e-06
HIGHEST = lax.Precision.HIGHEST
F32 = jnp.float32
BF16 = jnp.bfloat16
HALF = 64
RADIX = 256
VMEM_GRANT = 63963136


def nt(left, right):
    return lax.dot_general(
        left, right, (((1,), (1,)), ((), ())), preferred_element_type=F32
    )


def mm(left, right):
    return jnp.dot(left, right, preferred_element_type=F32)


def mm_full(left, right):
    return jnp.dot(left, right, preferred_element_type=F32, precision=HIGHEST)


def split(value):
    high = value.astype(BF16)
    return high, (value - high.astype(F32)).astype(BF16)


def complex_low(ar, ai, br, bi):
    a = jnp.concatenate([ar.astype(BF16), ai.astype(BF16)], axis=0)
    u = mm(a, br.astype(BF16))
    v = mm(a, bi.astype(BF16))
    n = ar.shape[0]
    return u[:n] - v[n:], u[n:] + v[:n]


def complex_split(ar, ai, br, bi):
    ar_high, ar_low = split(ar)
    ai_high, ai_low = split(ai)
    br_high, br_low = split(br)
    bi_high, bi_low = split(bi)
    n = ar.shape[0]
    a = jnp.concatenate([ar_high, ai_high, ar_low, ai_low], axis=0)
    a_high = jnp.concatenate([ar_high, ai_high], axis=0)
    u = mm(a, br_high)
    v = mm(a, bi_high)
    u_low = mm(a_high, br_low)
    v_low = mm(a_high, bi_low)
    rr = u[2 * n : 3 * n] + u_low[:n]
    ir = u[3 * n :] + u_low[n:]
    ri = v[2 * n : 3 * n] + v_low[:n]
    ii = v[3 * n :] + v_low[n:]
    return (u[:n] - v[n : 2 * n]) + (rr - ii), (u[n : 2 * n] + v[:n]) + (ir + ri)


def complex_full(ar, ai, br, bi):
    return (
        mm_full(ar, br) - mm_full(ai, bi),
        mm_full(ar, bi) + mm_full(ai, br),
    )


def newton_step(first, second, br, bi, xr, xi, eye, scale):
    yr = xr * scale
    yi = xi * scale
    tr, ti = first(br, bi, yr, yi)
    rr = eye - tr
    ri = -ti
    dr, di = second(yr, yi, rr, ri)
    return yr + dr, yi + di, rr, ri


def bound_after(low, high):
    spread = (high - low) / (high + low)
    return 1.0 - spread * spread


def precode_kernel(pieces, cell_width, shared, own_ref, other_ref, serving_ref, mask_ref, out_ref):
    me = lax.axis_index("cell")
    group = me if shared else pl.program_id(0)
    at = me if shared else 0
    users = own_ref.shape[2]
    width = own_ref.shape[3]
    row = lax.broadcasted_iota(jnp.int32, (users, users), 0)
    col = lax.broadcasted_iota(jnp.int32, (users, users), 1)
    diagonal = row == col
    eye = diagonal.astype(F32)

    def to_row(column):
        return jnp.sum(eye * column, axis=0, keepdims=True)

    def to_column(line):
        return jnp.sum(eye * line, axis=1, keepdims=True)

    serving = to_column(serving_ref[...].astype(F32))
    real_list, imag_list, own_real, own_imag = [], [], [], []
    for i in range(pieces):
        real = own_ref[0, at] if i == 0 else other_ref[i - 1, 0, 0]
        imag = own_ref[1, at] if i == 0 else other_ref[i - 1, 1, 0]
        start = lax.rem(me + i, pieces) * width
        antenna = start + lax.broadcasted_iota(jnp.int32, (users, width), 1)
        served = (antenna // cell_width).astype(F32) == serving
        real_list.append(real)
        imag_list.append(imag)
        own_real.append(jnp.where(served, real.astype(F32), 0.0).astype(BF16))
        own_imag.append(jnp.where(served, imag.astype(F32), 0.0).astype(BF16))
    hr = jnp.concatenate(real_list, axis=1)
    hi = jnp.concatenate(imag_list, axis=1)
    por = jnp.concatenate(own_real, axis=1)
    poi = jnp.concatenate(own_imag, axis=1)
    prod_r = nt(hr, por) + nt(hi, poi)
    prod_i = nt(hi, por) - nt(hr, poi)
    gram_r = nt(hr, hr) + nt(hi, hi)
    gram_i = nt(hi, hr) - nt(hr, hi)
    active_row = mask_ref[pl.ds(group, 1), :].astype(F32)
    active_col = to_column(active_row)
    size_row = jnp.sum(prod_r * eye, axis=0, keepdims=True)
    col_scale = active_row / jnp.sqrt(size_row + SMALL_FLOOR)
    eff_r = prod_r * col_scale
    eff_i = prod_i * col_scale
    power = eff_r * eff_r + eff_i * eff_i
    overall = jnp.sum(power, axis=1, keepdims=True) + NOISE
    interference = jnp.sum(jnp.where(diagonal, 0.0, power), axis=1, keepdims=True) + NOISE
    direct = jnp.sum(eff_r * eye, axis=1, keepdims=True)
    weight_root = jnp.sqrt(overall / interference)
    mix = weight_root * (direct / overall) * active_col
    gram_diag = jnp.sum(gram_r * eye, axis=1, keepdims=True)
    inner_diag = mix * mix * gram_diag + REGUL
    unit = lax.rsqrt(inner_diag)
    left = mix * unit
    right = to_row(left)
    br = jnp.where(diagonal, 1.0, gram_r * left * right)
    bi = gram_i * left * right
    upper = jnp.max(jnp.sum(jnp.sqrt(br * br + bi * bi), axis=1, keepdims=True))
    lower = REGUL / jnp.max(inner_diag)
    mild = lower > 0.01 * upper

    scale = 2.0 / (lower + upper)
    xr = scale * (2.0 * eye - scale * br)
    xi = -scale * scale * bi

    def quick_cond(state):
        return jnp.logical_and(mild, 1.0 - state[0] > 0.02)

    def quick_body(state):
        low, xr, xi = state
        xr, xi, _, _ = newton_step(
            complex_low, complex_low, br, bi, xr, xi, eye, 2.0 / (low + 1.0)
        )
        return bound_after(low, 1.0), xr, xi

    low, xr, xi = lax.while_loop(quick_cond, quick_body, (bound_after(lower, upper), xr, xi))
    low = jnp.where(mild, 1.0, low)

    def close_cond(state):
        return jnp.logical_and(mild, jnp.logical_and(state[0] > 0.003, state[1] < 3))

    def close_body(state):
        _, count, xr, xi = state
        xr, xi, rr, ri = newton_step(
            complex_split, complex_low, br, bi, xr, xi, eye, 1.0
        )
        return jnp.sum(rr * rr + ri * ri), count + 1, xr, xi

    remains, _, xr, xi = lax.while_loop(
        close_cond, close_body, (jnp.float32(1.0), jnp.int32(0), xr, xi)
    )

    def full_cond(state):
        return jnp.logical_and(state[1] > 0.003, state[2] < 40)

    def full_body(state):
        low, _, count, xr, xi = state
        xr, xi, rr, ri = newton_step(
            complex_full, complex_full, br, bi, xr, xi, eye, 2.0 / (low + 1.0)
        )
        return bound_after(low, 1.0), jnp.sum(rr * rr + ri * ri), count + 1, xr, xi

    _, _, _, xr, xi = lax.while_loop(
        full_cond, full_body, (low, remains, jnp.int32(0), xr, xi)
    )
    front = weight_root * unit
    yr_high, yr_low = split(xr * front * right)
    yi_high, yi_low = split(xi * front * right)
    if shared:
        for i, part in enumerate((yr_high, yi_high, yr_low, yi_low)):
            out_ref[i] = part
    else:
        pr, pi = finish((yr_high, yi_high, yr_low, yi_low), hr, hi)
        out_ref[0, 0] = pr[:, :width]
        out_ref[0, 1] = pi[:, :width]


def finish(factors, hr, hi):
    yr_high, yi_high, yr_low, yi_low = factors
    qr = (mm(yr_high, hr) - mm(yi_high, hi)) + (mm(yr_low, hr) - mm(yi_low, hi))
    qi = (mm(yr_high, hi) + mm(yi_high, hr)) + (mm(yr_low, hi) + mm(yi_low, hr))
    strength = jnp.sum(qr * qr + qi * qi, keepdims=True)
    scale = jnp.sqrt(hr.shape[1] / (strength + SMALL_FLOOR))
    return (qr * scale).astype(BF16), (qi * -scale).astype(BF16)


def swap_kernel(channel_ref, near_ref, swap_sems):
    sc = lax.axis_index("sc")
    core = lax.axis_index("cell")
    barrier = pltpu.get_barrier_semaphore()
    pl.semaphore_signal(
        barrier, inc=1, device_id=(sc, 1 - core), device_id_type=pl.DeviceIdType.MESH
    )
    pl.semaphore_wait(barrier, 1)
    swap = pltpu.make_async_remote_copy(
        src_ref=channel_ref.at[:, 1 - core],
        dst_ref=near_ref,
        send_sem=swap_sems.at[0],
        recv_sem=swap_sems.at[1],
        device_id=(sc, 1 - core),
        device_id_type=pl.DeviceIdType.MESH,
    )
    swap.start()
    swap.wait()


def swap_groups(channel):
    far = pl.BlockSpec(memory_space=pl.ANY)
    return pl.pallas_call(
        swap_kernel,
        out_shape=jax.ShapeDtypeStruct((2,) + channel.shape[2:], BF16),
        in_specs=[far],
        out_specs=far,
        scratch_shapes=[pltpu.SemaphoreType.DMA((2,))],
        compiler_params=pltpu.CompilerParams(collective_id=1, has_side_effects=True),
        name="swap_groups",
    )(channel)


def precode(channel, others, serving, mask, pieces, shared):
    groups = channel.shape[1]
    users = channel.shape[2]
    width = channel.shape[3]
    params = pltpu.CompilerParams(vmem_limit_bytes=VMEM_GRANT)
    kernel = functools.partial(precode_kernel, pieces, CELL_ANTENNAS, shared)
    if shared:
        whole = pl.BlockSpec(memory_space=pltpu.VMEM)
        return pl.pallas_call(
            kernel,
            out_shape=jax.ShapeDtypeStruct((4, users, users), BF16),
            in_specs=[whole] * 4,
            out_specs=whole,
            compiler_params=params,
            name="precode",
        )(channel, others, serving, mask)
    return pl.pallas_call(
        kernel,
        grid=(groups,),
        out_shape=jax.ShapeDtypeStruct((groups, 2, users, width), BF16),
        in_specs=[
            pl.BlockSpec((2, 1, users, width), lambda g: (0, g, 0, 0)),
            pl.BlockSpec((pieces - 1, 2, 1, users, width), lambda g: (0, 0, g, 0, 0)),
            pl.BlockSpec((1, users), lambda g: (0, 0)),
            pl.BlockSpec((groups, users), lambda g: (0, 0)),
        ],
        out_specs=pl.BlockSpec((1, 2, users, width), lambda g: (g, 0, 0, 0)),
        compiler_params=params,
        name="precode",
    )(channel, others, serving, mask)

def fft_tables(length):
    radix = length // RADIX
    q = np.arange(RADIX)
    back, forth = [], []
    for n1 in range(radix):
        angle = 2.0 * np.pi * ((q[:, None] * (radix * q[None, :] + n1)) % length) / length
        cos, sin = np.cos(angle), np.sin(angle)
        back.append(np.concatenate([cos.T, sin.T], axis=0))
        forth.append(np.concatenate([cos, sin], axis=0))
    return jnp.asarray(np.stack(back + forth), BF16)


def weighted(values, turned, radix, n, sign):
    total = None
    for r in range(radix):
        step = (r * n) % radix
        cos = math.cos(2.0 * math.pi * step / radix)
        sin = sign * math.sin(2.0 * math.pi * step / radix)
        for factor, piece in ((cos, values[r]), (sin, turned[r])):
            if abs(factor) < 1e-9:
                continue
            if abs(factor - 1.0) < 1e-9:
                term = piece
            elif abs(factor + 1.0) < 1e-9:
                term = -piece
            else:
                term = factor * piece
            total = term if total is None else total + term
    return total


def clip_transform(length, in_ref, table_ref, out_ref):
    radix = length // RADIX
    lanes = 2 * HALF
    sign = jnp.where(
        lax.broadcasted_iota(jnp.int32, (RADIX, lanes), 1) < HALF, -1.0, 1.0
    )

    def turn(value):
        return pltpu.roll(value, HALF, 1) * sign

    norm = 1.0 / math.sqrt(length)
    blocks = [in_ref[pl.ds(r * RADIX, RADIX), :].astype(F32) for r in range(radix)]
    turned = [turn(b) for b in blocks]
    waves, powers = [], []
    energy = jnp.zeros((1, lanes), F32)
    for n in range(radix):
        mixed = weighted(blocks, turned, radix, n, 1.0).astype(BF16)
        both = mm(table_ref[n], mixed)
        wave = (both[:RADIX] + turn(both[RADIX:])) * norm
        square = wave * wave
        power = square + pltpu.roll(square, HALF, 1)
        energy = energy + jnp.sum(power, axis=0, keepdims=True)
        waves.append(wave)
        powers.append(power)
    limit_square = CLIP_RATIO * CLIP_RATIO * (energy * (1.0 / length) + SMALL_FLOOR)
    limit = jnp.sqrt(limit_square) * norm
    spectra = []
    for n in range(radix):
        clipped = waves[n] * (limit * lax.rsqrt(jnp.maximum(powers[n], limit_square)))
        both = mm(table_ref[radix + n], clipped.astype(BF16))
        spectra.append(both[:RADIX] - turn(both[RADIX:]))
    turned = [turn(b) for b in spectra]
    for r in range(radix):
        out_ref[pl.ds(r * RADIX, RADIX), :] = weighted(
            spectra, turned, radix, r, -1.0
        ).astype(BF16)


def exchange_kernel(parts, shared, *refs):
    if shared:
        factors_far, channel_far, near_far = refs[:3]
        refs = refs[3:]
        width = near_far.shape[2]
        groups = 2
    else:
        mine_ref = refs[0]
        refs = refs[1:]
        width = mine_ref.shape[3]
        groups = mine_ref.shape[0]
    (
        data_far,
        table_far,
        out_ref,
        theirs_ref,
        other_ref,
        send_ref,
        recv_ref,
        spec_ref,
        ret_ref,
        data_ref,
        table_ref,
        factors_ref,
        own_ref,
        near_ref,
        table_sems,
        swap_sems,
        send_sems,
        recv_sems,
        back_send,
        back_recv,
    ) = refs
    me = lax.axis_index("sc")
    core = lax.axis_index("cell")
    length = recv_ref.shape[0]
    active = send_ref.shape[0]
    slots = data_ref.shape[1]
    tones = data_ref.shape[2]
    users = data_ref.shape[3]
    halves = width // HALF
    per = tones // groups
    mesh_ids = pl.DeviceIdType.MESH
    barrier = pltpu.get_barrier_semaphore()

    @pl.loop(1, parts)
    def _(k):
        pl.semaphore_signal(
            barrier, inc=1, device_id=(lax.rem(me + k, parts), core), device_id_type=mesh_ids
        )

    if shared:
        pl.semaphore_signal(barrier, inc=1, device_id=(me, 1 - core), device_id_type=mesh_ids)

    load_data = pltpu.make_async_copy(data_far, data_ref, table_sems.at[0])
    load_table = pltpu.make_async_copy(table_far, table_ref, table_sems.at[1])
    if shared:
        loads = [
            pltpu.make_async_copy(channel_far.at[:, core], own_ref, table_sems.at[2]),
            pltpu.make_async_copy(near_far, near_ref, table_sems.at[3]),
            pltpu.make_async_copy(factors_far, factors_ref, table_sems.at[4]),
        ]
        for copy in loads:
            copy.start()
    load_data.start()
    load_table.start()

    def emit(group, pr, pi):
        top, bottom = [], []
        for h in range(halves):
            cut = slice(h * HALF, (h + 1) * HALF)
            top += [pr[:, cut], pi[:, cut]]
            bottom += [-pi[:, cut], pr[:, cut]]
        top = jnp.concatenate(top, axis=1)
        bottom = jnp.concatenate(bottom, axis=1)
        start = pl.multiple_of(group * per, per)
        letters_r = data_ref[0, :, pl.ds(start, per), :].reshape(slots * per, users)
        letters_i = data_ref[1, :, pl.ds(start, per), :].reshape(slots * per, users)
        signal = (mm(letters_r, top) + mm(letters_i, bottom)).astype(BF16)
        for s in range(slots):
            for h in range(halves):
                send_ref[s * halves + h, pl.ds(start, per), :] = signal[
                    s * per : (s + 1) * per, h * 2 * HALF : (h + 1) * 2 * HALF
                ]

    def outward(group, target, origin):
        start = pl.multiple_of(group * per, per)
        place = pl.multiple_of(origin * tones + group * per, per)
        return pltpu.make_async_remote_copy(
            src_ref=send_ref.at[target, pl.ds(start, per)],
            dst_ref=recv_ref.at[pl.ds(place, per)],
            send_sem=send_sems.at[group, target],
            recv_sem=recv_sems.at[group, origin],
            device_id=(target, core),
            device_id_type=mesh_ids,
        )

    def send_group(group):
        @pl.loop(0, parts)
        def _(k):
            target = lax.rem(me + parts // 2 + k, parts)

            @pl.when(jnp.logical_and(target < active, target != me))
            def _():
                outward(group, target, me).start()

        @pl.when(me < active)
        def _():
            start = pl.multiple_of(group * per, per)
            place = pl.multiple_of(me * tones + group * per, per)
            recv_ref[pl.ds(place, per), :] = send_ref[me, pl.ds(start, per), :]

    if shared:
        for copy in loads:
            copy.wait()
        hr = jnp.concatenate([own_ref[0], near_ref[0]], axis=1)
        hi = jnp.concatenate([own_ref[1], near_ref[1]], axis=1)
        pr, pi = finish([factors_ref[i] for i in range(4)], hr, hi)
        theirs_ref[0] = pr[:, width:]
        theirs_ref[1] = pi[:, width:]
        load_data.wait()
        emit(core, pr[:, :width], pi[:, :width])
        pl.semaphore_wait(barrier, parts)
        swap = pltpu.make_async_remote_copy(
            src_ref=theirs_ref,
            dst_ref=other_ref,
            send_sem=swap_sems.at[0],
            recv_sem=swap_sems.at[1],
            device_id=(me, 1 - core),
            device_id_type=mesh_ids,
        )
        swap.start()
        send_group(core)
        swap.wait()
        emit(1 - core, other_ref[0], other_ref[1])
        send_group(1 - core)
    else:
        load_data.wait()
        for g in range(groups):
            emit(g, mine_ref[g, 0], mine_ref[g, 1])
        pl.semaphore_wait(barrier, parts - 1)
        for g in range(groups):
            send_group(g)

    def homeward(target, origin):
        place = pl.multiple_of(target * tones, tones)
        return pltpu.make_async_remote_copy(
            src_ref=spec_ref.at[pl.ds(place, tones)],
            dst_ref=ret_ref.at[origin],
            send_sem=back_send.at[target],
            recv_sem=back_recv.at[origin],
            device_id=(target, core),
            device_id_type=mesh_ids,
        )

    load_table.wait()

    @pl.when(me < active)
    def _():
        @pl.loop(1, parts)
        def _(k):
            origin = lax.rem(me + k, parts)
            for g in range(groups):
                outward(g, me, origin).wait_recv()

        clip_transform(length, recv_ref, table_ref, spec_ref)

        @pl.loop(0, parts)
        def _(k):
            target = lax.rem(me + parts // 2 + k, parts)

            @pl.when(target != me)
            def _():
                homeward(target, me).start()

        ret_ref[me] = spec_ref[pl.ds(pl.multiple_of(me * tones, tones), tones), :]

    for s in range(slots):
        for h in range(halves):

            @pl.when(me != s * halves + h)
            def _():
                homeward(me, s * halves + h).wait_recv()

        pieces = [ret_ref[s * halves + h] for h in range(halves)]
        for c in range(2):
            out_ref[c, s] = jnp.concatenate(
                [p[:, c * HALF : (c + 1) * HALF] for p in pieces], axis=1
            )

    @pl.loop(1, parts)
    def _(k):
        target = lax.rem(me + k, parts)

        @pl.when(target < active)
        def _():
            for g in range(groups):
                outward(g, target, me).wait_send()

        @pl.when(me < active)
        def _():
            homeward(target, me).wait_send()


def exchange(precoding, data_letters, parts, width, shared):
    slots, tones = data_letters.shape[1], data_letters.shape[2]
    users = data_letters.shape[3]
    length = parts * tones
    active = slots * (width // HALF)
    groups = 2 if shared else precoding[0].shape[0]
    table = fft_tables(length)
    whole = pl.BlockSpec(memory_space=pltpu.VMEM)
    dma = pltpu.SemaphoreType.DMA
    return pl.pallas_call(
        functools.partial(exchange_kernel, parts, shared),
        out_shape=jax.ShapeDtypeStruct((2, slots, tones, width), BF16),
        in_specs=[pl.BlockSpec(memory_space=pl.ANY) if shared else whole] * len(precoding)
        + [pl.BlockSpec(memory_space=pl.ANY)] * 2,
        out_specs=whole,
        scratch_shapes=[
            pltpu.VMEM((2, users, width), BF16),
            pltpu.VMEM((2, users, width), BF16),
            pltpu.VMEM((active, tones, 2 * HALF), BF16),
            pltpu.VMEM((length, 2 * HALF), BF16),
            pltpu.VMEM((length, 2 * HALF), BF16),
            pltpu.VMEM((active, tones, 2 * HALF), BF16),
            pltpu.VMEM(data_letters.shape, BF16),
            pltpu.VMEM(table.shape, BF16),
            pltpu.VMEM((4, users, users), BF16),
            pltpu.VMEM((2, users, width), BF16),
            pltpu.VMEM((2, users, width), BF16),
            dma((5,)),
            dma((2,)),
            dma((groups, active)),
            dma((groups, parts)),
            dma((parts,)),
            dma((active,)),
        ],
        compiler_params=pltpu.CompilerParams(
            collective_id=0, has_side_effects=True, vmem_limit_bytes=VMEM_GRANT
        ),
        name="exchange",
    )(*precoding, data_letters, table)


def body(channel, data_letters, serving, assigned_mask):
    parts = lax.axis_size("sc")
    pieces = lax.axis_size("cell")
    shared = pieces == 2 and channel.shape[1] == 2
    serving = serving[None, :]
    width = channel.shape[3]
    if shared:
        near = swap_groups(channel)
        factors = precode(channel, near[None, :, None], serving, assigned_mask, pieces, True)
        return exchange((factors, channel, near), data_letters, parts, width, True)
    others = [
        lax.ppermute(channel, "cell", [((i + k) % pieces, i) for i in range(pieces)])
        for k in range(1, pieces)
    ]
    mine = precode(channel, jnp.stack(others), serving, assigned_mask, pieces, False)
    return exchange((mine,), data_letters, parts, width, False)


def solution(mesh):
    return jax.shard_map(
        body,
        mesh=mesh,
        in_specs=(P(None, "sc", None, "cell"), P(None, None, "sc", None), P(), P("sc", None)),
        out_specs=P(None, None, "sc", "cell"),
        check_vma=False,
    )
```

```python
import functools
import math

import jax
import jax.numpy as jnp
import numpy as np
from jax import lax
from jax.experimental import pallas as pl
from jax.experimental.pallas import tpu as pltpu
from jax.sharding import PartitionSpec as P

CELL_ANTENNAS = 64
NOISE = 0.1
REGUL = 0.5
CLIP_RATIO = 1.5
SMALL_FLOOR = 1e-06
HIGHEST = lax.Precision.HIGHEST
F32 = jnp.float32
BF16 = jnp.bfloat16
HALF = 64
RADIX = 256
VMEM_GRANT = 63963136
EXCHANGE_GRANT = 63963136


def nt(left, right):
    return lax.dot_general(
        left, right, (((1,), (1,)), ((), ())), preferred_element_type=F32
    )


def mm(left, right):
    return jnp.dot(left, right, preferred_element_type=F32)


def mm_full(left, right):
    return jnp.dot(left, right, preferred_element_type=F32, precision=HIGHEST)


def split(value):
    high = value.astype(BF16)
    return high, (value - high.astype(F32)).astype(BF16)


def complex_low(ar, ai, br, bi):
    a = jnp.concatenate([ar.astype(BF16), ai.astype(BF16)], axis=0)
    u = mm(a, br.astype(BF16))
    v = mm(a, bi.astype(BF16))
    n = ar.shape[0]
    return u[:n] - v[n:], u[n:] + v[:n]


def complex_split(ar, ai, br, bi):
    ar_high, ar_low = split(ar)
    ai_high, ai_low = split(ai)
    br_high, br_low = split(br)
    bi_high, bi_low = split(bi)
    n = ar.shape[0]
    a = jnp.concatenate([ar_high, ai_high, ar_low, ai_low], axis=0)
    a_high = jnp.concatenate([ar_high, ai_high], axis=0)
    u = mm(a, br_high)
    v = mm(a, bi_high)
    u_low = mm(a_high, br_low)
    v_low = mm(a_high, bi_low)
    rr = u[2 * n : 3 * n] + u_low[:n]
    ir = u[3 * n :] + u_low[n:]
    ri = v[2 * n : 3 * n] + v_low[:n]
    ii = v[3 * n :] + v_low[n:]
    return (u[:n] - v[n : 2 * n]) + (rr - ii), (u[n : 2 * n] + v[:n]) + (ir + ri)


def complex_full(ar, ai, br, bi):
    return (
        mm_full(ar, br) - mm_full(ai, bi),
        mm_full(ar, bi) + mm_full(ai, br),
    )


def newton_step(first, second, br, bi, xr, xi, eye, scale):
    yr = xr * scale
    yi = xi * scale
    tr, ti = first(br, bi, yr, yi)
    rr = eye - tr
    ri = -ti
    dr, di = second(yr, yi, rr, ri)
    return yr + dr, yi + di, rr, ri


def bound_after(low, high):
    spread = (high - low) / (high + low)
    return 1.0 - spread * spread


def precode_kernel(pieces, cell_width, shared, own_ref, other_ref, serving_ref, mask_ref, out_ref, *scratch):
    me = lax.axis_index("cell")
    group = me if shared else pl.program_id(0)
    at = 0
    loads = []
    if shared:
        far = (own_ref.at[:, pl.ds(me, 1)], other_ref, serving_ref, mask_ref)
        own_ref, other_ref, serving_ref, mask_ref, sems = scratch
        near = (own_ref, other_ref, serving_ref, mask_ref)
        for i in range(4):
            copy = pltpu.make_async_copy(far[i], near[i], sems.at[i])
            copy.start()
            loads.append(copy)
    users = own_ref.shape[2]
    width = own_ref.shape[3]
    row = lax.broadcasted_iota(jnp.int32, (users, users), 0)
    col = lax.broadcasted_iota(jnp.int32, (users, users), 1)
    diagonal = row == col
    eye = diagonal.astype(F32)

    def to_row(column):
        return jnp.sum(eye * column, axis=0, keepdims=True)

    def to_column(line):
        return jnp.sum(eye * line, axis=1, keepdims=True)

    for copy in loads:
        copy.wait()
    serving = to_column(serving_ref[...].astype(F32))
    real_list, imag_list, own_real, own_imag = [], [], [], []
    for i in range(pieces):
        real = own_ref[0, at] if i == 0 else other_ref[i - 1, 0, 0]
        imag = own_ref[1, at] if i == 0 else other_ref[i - 1, 1, 0]
        start = lax.rem(me + i, pieces) * width
        antenna = start + lax.broadcasted_iota(jnp.int32, (users, width), 1)
        served = (antenna // cell_width).astype(F32) == serving
        real_list.append(real)
        imag_list.append(imag)
        own_real.append(jnp.where(served, real.astype(F32), 0.0).astype(BF16))
        own_imag.append(jnp.where(served, imag.astype(F32), 0.0).astype(BF16))
    hr = jnp.concatenate(real_list, axis=1)
    hi = jnp.concatenate(imag_list, axis=1)
    por = jnp.concatenate(own_real, axis=1)
    poi = jnp.concatenate(own_imag, axis=1)
    prod_r = nt(hr, por) + nt(hi, poi)
    prod_i = nt(hi, por) - nt(hr, poi)
    gram_r = nt(hr, hr) + nt(hi, hi)
    gram_i = nt(hi, hr) - nt(hr, hi)
    active_row = mask_ref[pl.ds(group, 1), :].astype(F32)
    active_col = to_column(active_row)
    size_row = jnp.sum(prod_r * eye, axis=0, keepdims=True)
    col_scale = active_row / jnp.sqrt(size_row + SMALL_FLOOR)
    eff_r = prod_r * col_scale
    eff_i = prod_i * col_scale
    power = eff_r * eff_r + eff_i * eff_i
    overall = jnp.sum(power, axis=1, keepdims=True) + NOISE
    interference = jnp.sum(jnp.where(diagonal, 0.0, power), axis=1, keepdims=True) + NOISE
    direct = jnp.sum(eff_r * eye, axis=1, keepdims=True)
    weight_root = jnp.sqrt(overall / interference)
    mix = weight_root * (direct / overall) * active_col
    gram_diag = jnp.sum(gram_r * eye, axis=1, keepdims=True)
    inner_diag = mix * mix * gram_diag + REGUL
    unit = lax.rsqrt(inner_diag)
    left = mix * unit
    right = to_row(left)
    br = jnp.where(diagonal, 1.0, gram_r * left * right)
    bi = gram_i * left * right
    upper = jnp.max(jnp.sum(jnp.sqrt(br * br + bi * bi), axis=1, keepdims=True))
    lower = REGUL / jnp.max(inner_diag)
    mild = lower > 0.01 * upper

    scale = 2.0 / (lower + upper)
    xr = scale * (2.0 * eye - scale * br)
    xi = -scale * scale * bi

    def quick_cond(state):
        return jnp.logical_and(mild, 1.0 - state[0] > 0.02)

    def quick_body(state):
        low, xr, xi = state
        xr, xi, _, _ = newton_step(
            complex_low, complex_low, br, bi, xr, xi, eye, 2.0 / (low + 1.0)
        )
        return bound_after(low, 1.0), xr, xi

    low, xr, xi = lax.while_loop(quick_cond, quick_body, (bound_after(lower, upper), xr, xi))
    low = jnp.where(mild, 1.0, low)

    def close_cond(state):
        return jnp.logical_and(mild, jnp.logical_and(state[0] > 0.003, state[1] < 3))

    def close_body(state):
        _, count, xr, xi = state
        xr, xi, rr, ri = newton_step(
            complex_split, complex_low, br, bi, xr, xi, eye, 1.0
        )
        return jnp.sum(rr * rr + ri * ri), count + 1, xr, xi

    remains, _, xr, xi = lax.while_loop(
        close_cond, close_body, (jnp.float32(1.0), jnp.int32(0), xr, xi)
    )

    def full_cond(state):
        return jnp.logical_and(state[1] > 0.003, state[2] < 40)

    def full_body(state):
        low, _, count, xr, xi = state
        xr, xi, rr, ri = newton_step(
            complex_full, complex_full, br, bi, xr, xi, eye, 2.0 / (low + 1.0)
        )
        return bound_after(low, 1.0), jnp.sum(rr * rr + ri * ri), count + 1, xr, xi

    _, _, _, xr, xi = lax.while_loop(
        full_cond, full_body, (low, remains, jnp.int32(0), xr, xi)
    )
    front = weight_root * unit
    yr_high, yr_low = split(xr * front * right)
    yi_high, yi_low = split(xi * front * right)
    if shared:
        for i, part in enumerate((yr_high, yi_high, yr_low, yi_low)):
            out_ref[i] = part
    else:
        pr, pi = finish((yr_high, yi_high, yr_low, yi_low), hr, hi)
        out_ref[0, 0] = pr[:, :width]
        out_ref[0, 1] = pi[:, :width]


def finish(factors, hr, hi):
    yr_high, yi_high, yr_low, yi_low = factors
    qr = (mm(yr_high, hr) - mm(yi_high, hi)) + (mm(yr_low, hr) - mm(yi_low, hi))
    qi = (mm(yr_high, hi) + mm(yi_high, hr)) + (mm(yr_low, hi) + mm(yi_low, hr))
    strength = jnp.sum(qr * qr + qi * qi, keepdims=True)
    scale = jnp.sqrt(hr.shape[1] / (strength + SMALL_FLOOR))
    return (qr * scale).astype(BF16), (qi * -scale).astype(BF16)


def swap_kernel(channel_ref, near_ref, swap_sems):
    sc = lax.axis_index("sc")
    core = lax.axis_index("cell")
    barrier = pltpu.get_barrier_semaphore()
    pl.semaphore_signal(
        barrier, inc=1, device_id=(sc, 1 - core), device_id_type=pl.DeviceIdType.MESH
    )
    pl.semaphore_wait(barrier, 1)
    swap = pltpu.make_async_remote_copy(
        src_ref=channel_ref.at[:, 1 - core],
        dst_ref=near_ref,
        send_sem=swap_sems.at[0],
        recv_sem=swap_sems.at[1],
        device_id=(sc, 1 - core),
        device_id_type=pl.DeviceIdType.MESH,
    )
    swap.start()
    swap.wait()


def swap_groups(channel):
    far = pl.BlockSpec(memory_space=pl.ANY)
    return pl.pallas_call(
        swap_kernel,
        out_shape=jax.ShapeDtypeStruct((2,) + channel.shape[2:], BF16),
        in_specs=[far],
        out_specs=far,
        scratch_shapes=[pltpu.SemaphoreType.DMA((2,))],
        compiler_params=pltpu.CompilerParams(collective_id=1, has_side_effects=True),
        name="swap_groups",
    )(channel)


def precode(channel, others, serving, mask, pieces, shared):
    groups = channel.shape[1]
    users = channel.shape[2]
    width = channel.shape[3]
    params = pltpu.CompilerParams(vmem_limit_bytes=VMEM_GRANT)
    kernel = functools.partial(precode_kernel, pieces, CELL_ANTENNAS, shared)
    if shared:
        whole = pl.BlockSpec(memory_space=pltpu.VMEM)
        return pl.pallas_call(
            kernel,
            out_shape=jax.ShapeDtypeStruct((4, users, users), BF16),
            in_specs=[pl.BlockSpec(memory_space=pl.ANY)] * 4,
            out_specs=whole,
            scratch_shapes=[
                pltpu.VMEM((2, 1, users, width), BF16),
                pltpu.VMEM(others.shape, BF16),
                pltpu.VMEM(serving.shape, serving.dtype),
                pltpu.VMEM(mask.shape, mask.dtype),
                pltpu.SemaphoreType.DMA((4,)),
            ],
            compiler_params=params,
            name="precode",
        )(channel, others, serving, mask)
    return pl.pallas_call(
        kernel,
        grid=(groups,),
        out_shape=jax.ShapeDtypeStruct((groups, 2, users, width), BF16),
        in_specs=[
            pl.BlockSpec((2, 1, users, width), lambda g: (0, g, 0, 0)),
            pl.BlockSpec((pieces - 1, 2, 1, users, width), lambda g: (0, 0, g, 0, 0)),
            pl.BlockSpec((1, users), lambda g: (0, 0)),
            pl.BlockSpec((groups, users), lambda g: (0, 0)),
        ],
        out_specs=pl.BlockSpec((1, 2, users, width), lambda g: (g, 0, 0, 0)),
        compiler_params=params,
        name="precode",
    )(channel, others, serving, mask)

def fft_tables(length):
    radix = length // RADIX
    q = np.arange(RADIX)
    back, forth = [], []
    for n1 in range(radix):
        angle = 2.0 * np.pi * ((q[:, None] * (radix * q[None, :] + n1)) % length) / length
        cos, sin = np.cos(angle), np.sin(angle)
        back.append(np.concatenate([cos.T, sin.T], axis=0))
        forth.append(np.concatenate([cos, sin], axis=0))
    return jnp.asarray(np.stack(back + forth), BF16)


def weighted(values, turned, radix, n, sign):
    total = None
    for r in range(radix):
        step = (r * n) % radix
        cos = math.cos(2.0 * math.pi * step / radix)
        sin = sign * math.sin(2.0 * math.pi * step / radix)
        for factor, piece in ((cos, values[r]), (sin, turned[r])):
            if abs(factor) < 1e-9:
                continue
            if abs(factor - 1.0) < 1e-9:
                term = piece
            elif abs(factor + 1.0) < 1e-9:
                term = -piece
            else:
                term = factor * piece
            total = term if total is None else total + term
    return total


def clip_transform(length, in_ref, table_ref, out_ref):
    radix = length // RADIX
    lanes = 2 * HALF
    sign = jnp.where(
        lax.broadcasted_iota(jnp.int32, (RADIX, lanes), 1) < HALF, -1.0, 1.0
    )

    def turn(value):
        return pltpu.roll(value, HALF, 1) * sign

    norm = 1.0 / math.sqrt(length)
    blocks = [in_ref[pl.ds(r * RADIX, RADIX), :].astype(F32) for r in range(radix)]
    turned = [turn(b) for b in blocks]
    waves, powers = [], []
    energy = jnp.zeros((1, lanes), F32)
    for n in range(radix):
        mixed = weighted(blocks, turned, radix, n, 1.0).astype(BF16)
        both = mm(table_ref[n], mixed)
        wave = (both[:RADIX] + turn(both[RADIX:])) * norm
        square = wave * wave
        power = square + pltpu.roll(square, HALF, 1)
        energy = energy + jnp.sum(power, axis=0, keepdims=True)
        waves.append(wave)
        powers.append(power)
    limit_square = CLIP_RATIO * CLIP_RATIO * (energy * (1.0 / length) + SMALL_FLOOR)
    limit = jnp.sqrt(limit_square) * norm
    spectra = []
    for n in range(radix):
        clipped = waves[n] * (limit * lax.rsqrt(jnp.maximum(powers[n], limit_square)))
        both = mm(table_ref[radix + n], clipped.astype(BF16))
        spectra.append(both[:RADIX] - turn(both[RADIX:]))
    turned = [turn(b) for b in spectra]
    for r in range(radix):
        out_ref[pl.ds(r * RADIX, RADIX), :] = weighted(
            spectra, turned, radix, r, -1.0
        ).astype(BF16)


def exchange_kernel(parts, shared, *refs):
    if shared:
        factors_far, channel_far, near_far = refs[:3]
        refs = refs[3:]
        width = near_far.shape[2]
        groups = 2
    else:
        mine_ref = refs[0]
        refs = refs[1:]
        width = mine_ref.shape[3]
        groups = mine_ref.shape[0]
    (
        data_far,
        table_far,
        ret_ref,
        theirs_ref,
        other_ref,
        send_ref,
        recv_ref,
        spec_ref,
        data_ref,
        table_ref,
        factors_ref,
        own_ref,
        near_ref,
        table_sems,
        swap_sems,
        send_sems,
        recv_sems,
        back_send,
        back_recv,
    ) = refs
    me = lax.axis_index("sc")
    core = lax.axis_index("cell")
    length = recv_ref.shape[0]
    active = send_ref.shape[0]
    slots = data_ref.shape[1]
    tones = data_ref.shape[2]
    users = data_ref.shape[3]
    halves = width // HALF
    per = tones // groups
    mesh_ids = pl.DeviceIdType.MESH
    barrier = pltpu.get_barrier_semaphore()

    @pl.loop(1, parts)
    def _(k):
        pl.semaphore_signal(
            barrier, inc=1, device_id=(lax.rem(me + k, parts), core), device_id_type=mesh_ids
        )

    if shared:
        pl.semaphore_signal(barrier, inc=1, device_id=(me, 1 - core), device_id_type=mesh_ids)

    load_data = pltpu.make_async_copy(data_far, data_ref, table_sems.at[0])
    load_table = pltpu.make_async_copy(table_far, table_ref, table_sems.at[1])
    if shared:
        loads = [
            pltpu.make_async_copy(channel_far.at[:, core], own_ref, table_sems.at[2]),
            pltpu.make_async_copy(near_far, near_ref, table_sems.at[3]),
            pltpu.make_async_copy(factors_far, factors_ref, table_sems.at[4]),
        ]
        for copy in loads:
            copy.start()
    load_data.start()
    load_table.start()

    def emit(group, pr, pi):
        top, bottom = [], []
        for h in range(halves):
            cut = slice(h * HALF, (h + 1) * HALF)
            top += [pr[:, cut], pi[:, cut]]
            bottom += [-pi[:, cut], pr[:, cut]]
        top = jnp.concatenate(top, axis=1)
        bottom = jnp.concatenate(bottom, axis=1)
        start = pl.multiple_of(group * per, per)
        letters_r = data_ref[0, :, pl.ds(start, per), :].reshape(slots * per, users)
        letters_i = data_ref[1, :, pl.ds(start, per), :].reshape(slots * per, users)
        signal = (mm(letters_r, top) + mm(letters_i, bottom)).astype(BF16)
        for s in range(slots):
            for h in range(halves):
                send_ref[s * halves + h, pl.ds(start, per), :] = signal[
                    s * per : (s + 1) * per, h * 2 * HALF : (h + 1) * 2 * HALF
                ]

    def outward(group, target, origin):
        start = pl.multiple_of(group * per, per)
        place = pl.multiple_of(origin * tones + group * per, per)
        return pltpu.make_async_remote_copy(
            src_ref=send_ref.at[target, pl.ds(start, per)],
            dst_ref=recv_ref.at[pl.ds(place, per)],
            send_sem=send_sems.at[group, target],
            recv_sem=recv_sems.at[group, origin],
            device_id=(target, core),
            device_id_type=mesh_ids,
        )

    def send_group(group):
        @pl.loop(0, parts)
        def _(k):
            target = lax.rem(me + parts // 2 + k, parts)

            @pl.when(jnp.logical_and(target < active, target != me))
            def _():
                outward(group, target, me).start()

        @pl.when(me < active)
        def _():
            start = pl.multiple_of(group * per, per)
            place = pl.multiple_of(me * tones + group * per, per)
            recv_ref[pl.ds(place, per), :] = send_ref[me, pl.ds(start, per), :]

    if shared:
        for copy in loads:
            copy.wait()
        hr = jnp.concatenate([own_ref[0], near_ref[0]], axis=1)
        hi = jnp.concatenate([own_ref[1], near_ref[1]], axis=1)
        pr, pi = finish([factors_ref[i] for i in range(4)], hr, hi)
        theirs_ref[0] = pr[:, width:]
        theirs_ref[1] = pi[:, width:]
        load_data.wait()
        emit(core, pr[:, :width], pi[:, :width])
        pl.semaphore_wait(barrier, parts)
        swap = pltpu.make_async_remote_copy(
            src_ref=theirs_ref,
            dst_ref=other_ref,
            send_sem=swap_sems.at[0],
            recv_sem=swap_sems.at[1],
            device_id=(me, 1 - core),
            device_id_type=mesh_ids,
        )
        swap.start()
        send_group(core)
        swap.wait()
        emit(1 - core, other_ref[0], other_ref[1])
        send_group(1 - core)
    else:
        load_data.wait()
        for g in range(groups):
            emit(g, mine_ref[g, 0], mine_ref[g, 1])
        pl.semaphore_wait(barrier, parts - 1)
        for g in range(groups):
            send_group(g)

    def homeward(target, origin):
        place = pl.multiple_of(target * tones, tones)
        return pltpu.make_async_remote_copy(
            src_ref=spec_ref.at[pl.ds(place, tones)],
            dst_ref=ret_ref.at[origin],
            send_sem=back_send.at[target],
            recv_sem=back_recv.at[origin],
            device_id=(target, core),
            device_id_type=mesh_ids,
        )

    load_table.wait()

    @pl.when(me < active)
    def _():
        @pl.loop(1, parts)
        def _(k):
            origin = lax.rem(me + k, parts)
            for g in range(groups):
                outward(g, me, origin).wait_recv()

        clip_transform(length, recv_ref, table_ref, spec_ref)

        @pl.loop(0, parts)
        def _(k):
            target = lax.rem(me + parts // 2 + k, parts)

            @pl.when(target != me)
            def _():
                homeward(target, me).start()

        keep = pltpu.make_async_copy(
            spec_ref.at[pl.ds(pl.multiple_of(me * tones, tones), tones)],
            ret_ref.at[me],
            table_sems.at[5],
        )
        keep.start()
        keep.wait()

    @pl.loop(0, active)
    def _(origin):
        @pl.when(me != origin)
        def _():
            homeward(me, origin).wait_recv()

    @pl.loop(1, parts)
    def _(k):
        target = lax.rem(me + k, parts)

        @pl.when(target < active)
        def _():
            for g in range(groups):
                outward(g, target, me).wait_send()

        @pl.when(me < active)
        def _():
            homeward(target, me).wait_send()


def exchange(precoding, data_letters, parts, width, shared):
    slots, tones = data_letters.shape[1], data_letters.shape[2]
    users = data_letters.shape[3]
    length = parts * tones
    active = slots * (width // HALF)
    groups = 2 if shared else precoding[0].shape[0]
    table = fft_tables(length)
    whole = pl.BlockSpec(memory_space=pltpu.VMEM)
    dma = pltpu.SemaphoreType.DMA
    received = pl.pallas_call(
        functools.partial(exchange_kernel, parts, shared),
        out_shape=jax.ShapeDtypeStruct((active, tones, 2 * HALF), BF16),
        in_specs=[pl.BlockSpec(memory_space=pl.ANY) if shared else whole] * len(precoding)
        + [pl.BlockSpec(memory_space=pl.ANY)] * 2,
        out_specs=pl.BlockSpec(memory_space=pl.ANY),
        scratch_shapes=[
            pltpu.VMEM((2, users, width), BF16),
            pltpu.VMEM((2, users, width), BF16),
            pltpu.VMEM((active, tones, 2 * HALF), BF16),
            pltpu.VMEM((length, 2 * HALF), BF16),
            pltpu.VMEM((length, 2 * HALF), BF16),
            pltpu.VMEM(data_letters.shape, BF16),
            pltpu.VMEM(table.shape, BF16),
            pltpu.VMEM((4, users, users), BF16),
            pltpu.VMEM((2, users, width), BF16),
            pltpu.VMEM((2, users, width), BF16),
            dma((6,)),
            dma((2,)),
            dma((groups, active)),
            dma((groups, parts)),
            dma((parts,)),
            dma((active,)),
        ],
        compiler_params=pltpu.CompilerParams(
            collective_id=0, has_side_effects=True, vmem_limit_bytes=EXCHANGE_GRANT
        ),
        name="exchange",
    )(*precoding, data_letters, table)
    return pl.pallas_call(
        functools.partial(spread_kernel, width // HALF),
        out_shape=jax.ShapeDtypeStruct((2, slots, tones, width), BF16),
        name="spread",
    )(received)


def spread_kernel(halves, in_ref, out_ref):
    for s in range(out_ref.shape[1]):
        pieces = [in_ref[s * halves + h] for h in range(halves)]
        for c in range(2):
            out_ref[c, s] = jnp.concatenate(
                [p[:, c * HALF : (c + 1) * HALF] for p in pieces], axis=1
            )


def body(channel, data_letters, serving, assigned_mask):
    parts = lax.axis_size("sc")
    pieces = lax.axis_size("cell")
    shared = pieces == 2 and channel.shape[1] == 2
    serving = serving[None, :]
    width = channel.shape[3]
    if shared:
        near = swap_groups(channel)
        factors = precode(channel, near[None, :, None], serving, assigned_mask, pieces, True)
        return exchange((factors, channel, near), data_letters, parts, width, True)
    others = [
        lax.ppermute(channel, "cell", [((i + k) % pieces, i) for i in range(pieces)])
        for k in range(1, pieces)
    ]
    mine = precode(channel, jnp.stack(others), serving, assigned_mask, pieces, False)
    return exchange((mine,), data_letters, parts, width, False)


def solution(mesh):
    return jax.shard_map(
        body,
        mesh=mesh,
        in_specs=(P(None, "sc", None, "cell"), P(None, None, "sc", None), P(), P("sc", None)),
        out_specs=P(None, None, "sc", "cell"),
        check_vma=False,
    )
```
